512 devices in a mesh: hid: 64 (over y, x, z_hi, core), mod: 8 (over z_lo).
Axes of the slice: x: 4, y: 4, z: 16 (z_hi: 2, z_lo: 8; z = z_hi * 8 + z_lo), core: 2. Of those that a mesh axis runs over, the one named last changes fastest.
Arguments:
- tokens: bfloat16 [512, 8192], P('hid', 'mod'), may hold values from -6 to 6
- cotangent: bfloat16 [512, 8192], P('hid', 'mod'), may hold values from -1.2578125 to 1.2578125
- gate_weight: bfloat16 [8192, 26624], P('mod', 'hid'), may hold values from -0.0625 to 0.0625
- up_weight: bfloat16 [8192, 26624], P('mod', 'hid'), may hold values from -0.0625 to 0.0625
- down_weight: bfloat16 [26624, 8192], P('hid', 'mod'), may hold values from -0.0390625 to 0.0390625
Outputs:
- grad_in: bfloat16 [512, 8192], P('hid', 'mod')
- grad_gate: bfloat16 [8192, 26624], P('mod', 'hid')
- grad_up: bfloat16 [8192, 26624], P('mod', 'hid')
- grad_down: bfloat16 [26624, 8192], P('hid', 'mod')
The draws below stay inside these ranges and needn't reach their ends.
All inputs are finite; a program needn't handle non-finite values.
Results may differ from the reference program's by a relative error of at most 0.027.
Values may be sent and summed in bfloat16 or wider, within the bound.
A program may use at most 64 MiB of HBM per device.

```python
import jax
import jax.numpy as jnp
from jax import lax

D = 8192
FF = 26624
TOKENS = 512
N_MOD = 8


def shard_levels(own_key, shape, split, least, largest):
    loudness = 1.0
    for position, shards_of in split:
        heights = jax.random.uniform(jax.random.fold_in(jax.random.fold_in(own_key, 6), position), (shards_of,), jnp.float32, least / len(split), largest / len(split))
        loudness = loudness * jnp.repeat(jnp.exp(heights), shape[position] // shards_of).reshape((-1,) + (1,) * (len(shape) - 1 - position))
    return loudness


def scatter_about(rng, extent, scale, most, pieces=(), kind=jnp.bfloat16):
    loudness = shard_levels(rng, extent, pieces, -0.22, 0.18) if pieces else 1.0
    entries = jax.random.normal(rng, extent, jnp.float32) * scale * loudness
    return jnp.minimum(jnp.maximum(entries, -most), most).astype(kind)


def setup_inputs(seed: int = 0) -> dict:
    arg_keys = jax.random.split(jax.random.key(seed), 6)
    tokens = scatter_about(arg_keys[0], (TOKENS, D), 1.0, 6.0, ((0, 64), (1, 8)))
    cotangent = scatter_about(arg_keys[1], (TOKENS, D), (TOKENS ** -0.25), 1.2578125, ((0, 64), (1, 8)))
    gate_weight = scatter_about(arg_keys[2], (D, FF), D ** -0.5, 0.0625, ((0, 8), (1, 64)))
    up_weight = scatter_about(arg_keys[3], (D, FF), D ** -0.5, 0.0625, ((0, 8), (1, 64)))
    down_weight = scatter_about(arg_keys[4], (FF, D), FF ** -0.5, 0.0390625, ((0, 64), (1, 8)))
    return dict(tokens=tokens, cotangent=cotangent, gate_weight=gate_weight, up_weight=up_weight, down_weight=down_weight)


readout_scale = 2.0


def block_sum(left, right):
    width = left.shape[1] // N_MOD
    total = jnp.zeros((left.shape[0], right.shape[1]), jnp.float32)
    for block in range(N_MOD):
        partial_sum = jnp.dot(left[:, block * width:(block + 1) * width], right[block * width:(block + 1) * width], preferred_element_type=jnp.float32)
        rounded = lax.optimization_barrier(partial_sum.astype(jnp.bfloat16))
        total = total + rounded.astype(jnp.float32)
    return total


def reference(tokens, cotangent, gate_weight, up_weight, down_weight):
    gate = block_sum(tokens, gate_weight)
    up = block_sum(tokens, up_weight)
    back = readout_scale * block_sum(cotangent, down_weight.T)
    sigmoid_gate = jax.nn.sigmoid(gate)
    activated = gate * sigmoid_gate
    hidden = (activated * up).astype(jnp.bfloat16)
    d_up = (back * activated).astype(jnp.bfloat16)
    d_gate = (back * up * sigmoid_gate * (1.0 + gate * (1.0 - sigmoid_gate))).astype(jnp.bfloat16)
    grad_down = (readout_scale * jnp.dot(hidden.T, cotangent, preferred_element_type=jnp.float32)).astype(jnp.bfloat16)
    grad_gate = jnp.dot(tokens.T, d_gate, preferred_element_type=jnp.float32).astype(jnp.bfloat16)
    grad_up = jnp.dot(tokens.T, d_up, preferred_element_type=jnp.float32).astype(jnp.bfloat16)
    grad_in = (jnp.dot(d_gate, gate_weight.T, preferred_element_type=jnp.float32) + jnp.dot(d_up, up_weight.T, preferred_element_type=jnp.float32)).astype(jnp.bfloat16)
    return grad_in, grad_gate, grad_up, grad_down
```

```python
import functools

import jax
import jax.numpy as jnp
from jax import lax
from jax.experimental import pallas as pl
from jax.experimental.pallas import tpu as pltpu
from jax.sharding import PartitionSpec as P

readout_scale = 2.0
N_MOD = 8
LAG = 2
ROWS = 32
MESH = pl.DeviceIdType.MESH
F32 = jnp.float32
BF16 = jnp.bfloat16


def swiglu_grads(gate, up, back):
    back = readout_scale * back
    sigmoid_gate = jax.nn.sigmoid(gate)
    activated = gate * sigmoid_gate
    hidden = (activated * up).astype(BF16)
    d_gate = (back * up * sigmoid_gate * (1.0 + gate * (1.0 - sigmoid_gate))).astype(BF16)
    d_up = (back * activated).astype(BF16)
    return hidden, d_gate, d_up


def kernel(
    tok_ref, cot_ref, wg_ref, wu_ref, wd_ref,
    gin_ref, gg_ref, gu_ref, gd_ref,
    xin, stage, full, wbuf, wt, part, redbuf, res, grad, sibbuf, rb1, a1, rb2, a2, rb3, outbuf, obuf,
    s0_send, s0_recv, ag_send, ag_recv, sib_send, sib_recv,
    red_send, red_recv, bc_send, bc_recv,
    r0_send, r0_recv, r1_send, r1_recv, r2_send, r2_recv, r3_send, r3_recv, r4_send, r4_recv,
    w_sem, o_sem,
):
    hid = lax.axis_index("hid")
    zl = lax.axis_index("mod")
    c = lax.rem(hid, 2)
    z = lax.rem(hid // 2, 2)
    x = lax.rem(hid // 4, 4)
    y = hid // 16
    chunks = part.shape[1]

    def dev(yy, xx, zz, cc):
        return (((yy * 4 + xx) * 2 + zz) * 2 + cc, zl)

    def coords(k_out, k_in):
        xx = lax.rem(x + k_in * (1 - c) + k_out * c, 4)
        yy = lax.rem(y + k_in * c + k_out * (1 - c), 4)
        return yy, xx

    def block(k_out, k_in):
        yy, xx = coords(k_out, k_in)
        return yy * 4 + xx

    def peer(k_out, k_in):
        yy, xx = coords(k_out, k_in)
        return dev(yy, xx, z, c)

    sibling = dev(y, x, z, 1 - c)

    def rcopy(src, dst, ssem, rsem, target):
        return pltpu.make_async_remote_copy(
            src_ref=src, dst_ref=dst, send_sem=ssem, recv_sem=rsem, device_id=target, device_id_type=MESH
        )

    w_copies = [
        pltpu.make_async_copy(wg_ref, wbuf.at[0], w_sem.at[0]),
        pltpu.make_async_copy(wu_ref, wbuf.at[1], w_sem.at[1]),
        pltpu.make_async_copy(wd_ref, wt.at[2], w_sem.at[2]),
    ]
    for copy in w_copies:
        copy.start()

    barrier = pltpu.get_barrier_semaphore()
    greeted = [sibling, dev(y, x, 1 - z, 0), dev(y, x, 1 - z, 1)]
    greeted += [peer(0, k) for k in (1, 2, 3)] + [peer(k, 0) for k in (1, 2, 3)]
    greeted += [(hid, lax.rem(zl + 1, N_MOD)), (hid, lax.rem(zl + N_MOD - 1, N_MOD))]
    for target in greeted:
        pl.semaphore_signal(barrier, inc=1, device_id=target, device_id_type=MESH)
    xin[0] = tok_ref[...]
    xin[1] = cot_ref[...]
    pl.semaphore_wait(barrier, len(greeted))

    slot = z * 2 + c
    first = [
        rcopy(xin.at[0], stage.at[slot], s0_send.at[0], s0_recv.at[slot], dev(y, x, 1 - z, 0)),
        rcopy(xin.at[1], stage.at[slot], s0_send.at[1], s0_recv.at[slot], dev(y, x, 1 - z, 1)),
        rcopy(xin.at[1 - c], stage.at[slot], s0_send.at[2], s0_recv.at[slot], sibling),
    ]
    for copy in first:
        copy.start()
    stage[slot] = xin[c]
    for other in (z * 2 + 1 - c, (1 - z) * 2, (1 - z) * 2 + 1):
        rcopy(xin.at[0], stage.at[other], s0_send.at[0], s0_recv.at[other], sibling).wait_recv()
    mine = y * 4 + x
    full[c, mine] = stage[...].astype(F32).reshape(32, stage.shape[2]).astype(BF16)

    def ag_copy(b, send_index, target):
        return rcopy(full.at[c, b], full.at[c, b], ag_send.at[send_index], ag_recv.at[b], target)

    def sib_copy(b):
        return rcopy(full.at[c, b], full.at[c, b], sib_send.at[b], sib_recv.at[b], sibling)

    for k in (1, 2, 3):
        ag_copy(mine, 12 + k - 1, peer(0, k)).start()
    for k in (1, 2, 3):
        ag_copy(mine, k - 1, peer(k, 0)).start()
    sib_copy(mine).start()

    for copy in w_copies:
        copy.wait()
    wt[0] = wbuf[0].T
    wt[1] = wbuf[1].T

    @pl.loop(1, 4)
    def _(k_in):
        b = block(0, 4 - k_in)
        ag_copy(b, 0, sibling).wait_recv()
        for k in (1, 2, 3):
            ag_copy(b, k_in * 3 + k - 1, peer(k, 0)).start()
        sib_copy(b).start()

    @pl.loop(0, 12)
    def _(j):
        b = block(4 - (1 + j % 3), lax.rem(4 - j // 3, 4))
        ag_copy(b, 0, sibling).wait_recv()
        sib_copy(b).start()

    @pl.loop(0, 16)
    def _(b):
        rcopy(full.at[1 - c, b], full.at[1 - c, b], sib_send.at[b], sib_recv.at[b], sibling).wait_recv()

    width = full.shape[3]
    for d in range(2):
        for i in range(3):
            acts = full[i // 2, d * 8:(d + 1) * 8].reshape(256, width)
            sums = lax.dot_general(wt[i], acts, (((1,), (1,)), ((), ())), preferred_element_type=F32)
            part[d, :, i] = sums.astype(BF16).reshape(chunks, ROWS, 256)

    last = N_MOD - 1

    def red_copy(d, k, target):
        return rcopy(part.at[d, k], redbuf.at[d, k], red_send.at[d, k], red_recv.at[d, k], (hid, target))

    def bc_copy(d, k, target):
        return rcopy(res.at[d, k], res.at[d, k], bc_send.at[d, k], bc_recv.at[d, k], (hid, target))

    @pl.loop(0, 2 * last * LAG + chunks)
    def _(step):
        for d in range(2):
            place = zl if d == 0 else last - zl
            ahead = jnp.minimum(zl + 1, last) if d == 0 else jnp.maximum(zl - 1, 0)
            behind = jnp.maximum(zl - 1, 0) if d == 0 else jnp.minimum(zl + 1, last)
            k = step - LAG * place
            live = (k >= 0) & (k < chunks)

            @pl.when(live & (place == 0))
            def _():
                red_copy(d, k, ahead).start()

            @pl.when(live & (place > 0) & (place < last))
            def _():
                red_copy(d, k, ahead).wait_recv()
                part[d, k] = (part[d, k].astype(F32) + redbuf[d, k].astype(F32)).astype(BF16)
                red_copy(d, k, ahead).start()

            @pl.when(live & (place == last))
            def _():
                red_copy(d, k, behind).wait_recv()
                sums = part[d, k].astype(F32) + redbuf[d, k].astype(F32)
                hidden, d_gate, d_up = swiglu_grads(sums[0], sums[1], sums[2])
                res[d, k, 0] = hidden
                res[d, k, 1] = d_gate
                res[d, k, 2] = d_up
                bc_copy(d, k, behind).start()

            kb = step - LAG * (2 * last - place)
            live_b = (kb >= 0) & (kb < chunks) & (place < last)

            @pl.when(live_b)
            def _():
                bc_copy(d, kb, behind).wait_recv()

                @pl.when(place > 0)
                def _():
                    bc_copy(d, kb, behind).start()

    half = width // 2
    hidden_units = chunks * ROWS

    def sib_grad(d):
        blocks = pl.ds(d * 8, 8)
        return rcopy(grad.at[1 - c, blocks], sibbuf.at[blocks], r0_send.at[d], r0_recv.at[d], sibling)

    for d in range(2):
        total = jnp.zeros((256, width), F32)
        for i in range(2):
            total += lax.dot_general(
                res[d, :, i + 1].reshape(hidden_units, 256), wt[i], (((0,), (0,)), ((), ())), preferred_element_type=F32
            )
        total = total.astype(BF16)
        for h in range(2):
            grad[h, d * 8:(d + 1) * 8] = total[:, h * half:(h + 1) * half].reshape(8, 32, half)
        sib_grad(d).start()

    def weight_grad(i, scale):
        total = jnp.zeros((hidden_units, width), F32)
        for d in range(2):
            acts = full[1 if i == 0 else 0, d * 8:(d + 1) * 8].reshape(256, width)
            total += jnp.dot(res[d, :, i].reshape(hidden_units, 256), acts, preferred_element_type=F32)
        if scale is not None:
            total = scale * total
        obuf[i] = total.astype(BF16)
        copy = pltpu.make_async_copy(obuf.at[i], (gd_ref, gg_ref, gu_ref)[i], o_sem.at[i])
        copy.start()
        return copy

    for d in range(2):
        sib_grad(d).wait_recv()
    for d in range(2):
        blocks = pl.ds(d * 8, 8)
        grad[c, blocks] = (grad[c, blocks].astype(F32) + sibbuf[blocks].astype(F32)).astype(BF16)

    def r1_copy(k_out, k_in):
        return rcopy(
            grad.at[c, block(k_out, k_in)], rb1.at[k_out - 1, k_in],
            r1_send.at[k_out - 1, k_in], r1_recv.at[k_out - 1, k_in], peer(k_out, 0),
        )

    def r2_copy(k_in):
        return rcopy(a1.at[k_in], rb2.at[k_in - 1], r2_send.at[k_in - 1], r2_recv.at[k_in - 1], peer(0, k_in))

    @pl.loop(1, 5)
    def _(j):
        k_in = lax.rem(j, 4)
        for k_out in (1, 2, 3):
            r1_copy(k_out, k_in).start()

    out_copies = [weight_grad(0, readout_scale)]

    for k_in in (1, 2, 3, 0):
        total = grad[c, block(0, k_in)].astype(F32)
        for k_out in (1, 2, 3):
            r1_copy(k_out, k_in).wait_recv()
        for k_out in (1, 2, 3):
            total += rb1[k_out - 1, k_in].astype(F32)
        a1[k_in] = total.astype(BF16)
        if k_in:
            r2_copy(k_in).start()

    out_copies.append(weight_grad(1, None))
    total = a1[0].astype(F32)
    for k_in in (1, 2, 3):
        r2_copy(k_in).wait_recv()
    for k_in in (1, 2, 3):
        total += rb2[k_in - 1].astype(F32)
    a2[...] = total.astype(BF16).reshape(2, 16, half)
    r3 = rcopy(a2.at[1 - z], rb3, r3_send, r3_recv, dev(y, x, 1 - z, c))
    r3.start()
    out_copies.append(weight_grad(2, None))
    r3.wait_recv()
    total = a2[z].astype(F32) + rb3[...].astype(F32)
    a3 = total.reshape(2, 8, half).astype(BF16)
    a1_out = outbuf
    a1_out[0] = a3
    r4 = rcopy(a1_out.at[0, 1 - c], a1_out.at[1, 0], r4_send, r4_recv, sibling)
    r4.start()
    r4.wait_recv()
    own = a1_out[0, c]
    theirs = a1_out[1, 0]
    is0 = c == 0
    gin_ref[:, :half] = jnp.where(is0, own, theirs)
    gin_ref[:, half:] = jnp.where(is0, theirs, own)

    for copy in first:
        copy.wait_send()

    @pl.loop(0, 15)
    def _(i):
        ag_copy(mine, i, sibling).wait_send()

    @pl.loop(0, 16)
    def _(b):
        sib_copy(b).wait_send()

    @pl.loop(0, chunks)
    def _(k):
        for d in range(2):
            place = zl if d == 0 else last - zl

            @pl.when(place < last)
            def _():
                red_copy(d, k, zl).wait_send()

            @pl.when(place > 0)
            def _():
                bc_copy(d, k, zl).wait_send()

    for d in range(2):
        sib_grad(d).wait_send()
    for k_in in range(4):
        for k_out in (1, 2, 3):
            r1_copy(k_out, k_in).wait_send()
        if k_in:
            r2_copy(k_in).wait_send()
    r3.wait_send()
    r4.wait_send()
    for copy in out_copies:
        copy.wait()


def local(tokens, cotangent, gate_weight, up_weight, down_weight):
    width = tokens.shape[1]
    units = down_weight.shape[0]
    chunks = units // ROWS
    half = width // 2
    dma = pltpu.SemaphoreType.DMA
    vmem = pl.BlockSpec(memory_space=pltpu.VMEM)
    hbm = pl.BlockSpec(memory_space=pl.ANY)
    grad_in, grad_gate, grad_up, grad_down = pl.pallas_call(
        kernel,
        out_shape=(
            jax.ShapeDtypeStruct(tokens.shape, BF16),
            jax.ShapeDtypeStruct((units, width), BF16),
            jax.ShapeDtypeStruct((units, width), BF16),
            jax.ShapeDtypeStruct((units, width), BF16),
        ),
        in_specs=[vmem, vmem, hbm, hbm, hbm],
        out_specs=(vmem, hbm, hbm, hbm),
        scratch_shapes=[
            pltpu.VMEM((2, 8, width), BF16),
            pltpu.VMEM((4, 8, width), BF16),
            pltpu.VMEM((2, 16, 32, width), BF16),
            pltpu.VMEM((2, width, units), BF16),
            pltpu.VMEM((3, units, width), BF16),
            pltpu.VMEM((2, chunks, 3, ROWS, 256), BF16),
            pltpu.VMEM((2, chunks, 3, ROWS, 256), BF16),
            pltpu.VMEM((2, chunks, 3, ROWS, 256), BF16),
            pltpu.VMEM((2, 16, 32, half), BF16),
            pltpu.VMEM((16, 32, half), BF16),
            pltpu.VMEM((3, 4, 32, half), BF16),
            pltpu.VMEM((4, 32, half), BF16),
            pltpu.VMEM((3, 32, half), BF16),
            pltpu.VMEM((2, 16, half), BF16),
            pltpu.VMEM((16, half), BF16),
            pltpu.VMEM((2, 2, 8, half), BF16),
            pltpu.VMEM((3, units, width), BF16),
            dma((3,)), dma((4,)), dma((15,)), dma((16,)), dma((16,)), dma((16,)),
            dma((2, chunks)), dma((2, chunks)), dma((2, chunks)), dma((2, chunks)),
            dma((2,)), dma((2,)), dma((3, 4)), dma((3, 4)), dma((3,)), dma((3,)),
            dma(()), dma(()), dma(()), dma(()),
            dma((3,)), dma((3,)),
        ],
        compiler_params=pltpu.CompilerParams(
            collective_id=0, has_side_effects=True, vmem_limit_bytes=48 * 1024 * 1024
        ),
    )(tokens, cotangent, gate_weight, up_weight, down_weight)
    return grad_in, grad_gate.T, grad_up.T, grad_down


def solution(mesh):
    placed = (P("hid", "mod"), P("hid", "mod"), P("mod", "hid"), P("mod", "hid"), P("hid", "mod"))
    return jax.shard_map(
        local,
        mesh=mesh,
        in_specs=placed,
        out_specs=(P("hid", "mod"), P("mod", "hid"), P("mod", "hid"), P("hid", "mod")),
        check_vma=False,
    )
```

```python
import functools

import jax
import jax.numpy as jnp
from jax import lax
from jax.experimental import pallas as pl
from jax.experimental.pallas import tpu as pltpu
from jax.sharding import PartitionSpec as P

readout_scale = 2.0
N_MOD = 8
LAG = 6
ROWS = 32
MESH = pl.DeviceIdType.MESH
F32 = jnp.float32
BF16 = jnp.bfloat16


def swiglu_grads(gate, up, back):
    back = readout_scale * back
    sigmoid_gate = jax.nn.sigmoid(gate)
    activated = gate * sigmoid_gate
    hidden = (activated * up).astype(BF16)
    d_gate = (back * up * sigmoid_gate * (1.0 + gate * (1.0 - sigmoid_gate))).astype(BF16)
    d_up = (back * activated).astype(BF16)
    return hidden, d_gate, d_up


def kernel(
    tok_ref, cot_ref, wg_ref, wu_ref, wd_ref,
    gin_ref, gg_ref, gu_ref, gd_ref,
    xin, stage, full, wt, part, redbuf, res, grad, sibbuf, rb1, a1, rb2, a2, rb3, outbuf, obuf,
    s0_send, s0_recv, ag_send, ag_recv, sib_send, sib_recv,
    red_send, red_recv, bc_send, bc_recv,
    r0_send, r0_recv, r1_send, r1_recv, r2_send, r2_recv, r3_send, r3_recv, r4_send, r4_recv,
    w_sem, o_sem,
):
    hid = lax.axis_index("hid")
    zl = lax.axis_index("mod")
    c = lax.rem(hid, 2)
    z = lax.rem(hid // 2, 2)
    x = lax.rem(hid // 4, 4)
    y = hid // 16
    chunks = part.shape[1]
    last = N_MOD - 1

    def dev(yy, xx, zz, cc):
        return (((yy * 4 + xx) * 2 + zz) * 2 + cc, zl)

    def coords(k_out, k_in):
        xx = lax.rem(x + k_in * (1 - c) + k_out * c, 4)
        yy = lax.rem(y + k_in * c + k_out * (1 - c), 4)
        return yy, xx

    def block(k_out, k_in):
        yy, xx = coords(k_out, k_in)
        return yy * 4 + xx

    def peer(k_out, k_in):
        yy, xx = coords(k_out, k_in)
        return dev(yy, xx, z, c)

    def quarter(q):
        return pl.ds(lax.rem(y + q, 4) * 4, 4)

    sibling = dev(y, x, z, 1 - c)

    def rcopy(src, dst, ssem, rsem, target):
        return pltpu.make_async_remote_copy(
            src_ref=src, dst_ref=dst, send_sem=ssem, recv_sem=rsem, device_id=target, device_id_type=MESH
        )

    barrier = pltpu.get_barrier_semaphore()
    greeted = [sibling, dev(y, x, 1 - z, 0), dev(y, x, 1 - z, 1)]
    greeted += [peer(0, k) for k in (1, 2, 3)] + [peer(k, 0) for k in (1, 2, 3)]
    for target in greeted:
        pl.semaphore_signal(barrier, inc=1, device_id=target, device_id_type=MESH)

    @pl.when(zl < last)
    def _():
        pl.semaphore_signal(barrier, inc=1, device_id=(hid, jnp.minimum(zl + 1, last)), device_id_type=MESH)

    @pl.when(zl > 0)
    def _():
        pl.semaphore_signal(barrier, inc=1, device_id=(hid, jnp.maximum(zl - 1, 0)), device_id_type=MESH)

    w_copies = [
        pltpu.make_async_copy(wg_ref, wt.at[0], w_sem.at[0]),
        pltpu.make_async_copy(wu_ref, wt.at[1], w_sem.at[1]),
        pltpu.make_async_copy(wd_ref, wt.at[2], w_sem.at[2]),
    ]
    for copy in w_copies:
        copy.start()
    xin[0] = tok_ref[...]
    xin[1] = cot_ref[...]
    pl.semaphore_wait(barrier, len(greeted) + jnp.minimum(zl, 1) + jnp.minimum(last - zl, 1))

    slot = z * 2 + c
    first = [
        rcopy(xin.at[0], stage.at[slot], s0_send.at[0], s0_recv.at[slot], dev(y, x, 1 - z, 0)),
        rcopy(xin.at[1], stage.at[slot], s0_send.at[1], s0_recv.at[slot], dev(y, x, 1 - z, 1)),
        rcopy(xin.at[1 - c], stage.at[slot], s0_send.at[2], s0_recv.at[slot], sibling),
    ]
    for copy in first:
        copy.start()
    stage[slot] = xin[c]
    for other in (z * 2 + 1 - c, (1 - z) * 2, (1 - z) * 2 + 1):
        rcopy(xin.at[0], stage.at[other], s0_send.at[0], s0_recv.at[other], sibling).wait_recv()
    mine = y * 4 + x
    full[c, mine] = stage[...].astype(F32).reshape(32, stage.shape[2]).astype(BF16)

    def ag_copy(b, target):
        return rcopy(full.at[c, b], full.at[c, b], ag_send, ag_recv.at[b], target)

    def sib_copy(b):
        return rcopy(full.at[c, b], full.at[c, b], sib_send, sib_recv.at[b], sibling)

    for k in (1, 2, 3):
        ag_copy(mine, peer(0, k)).start()
    for k in (1, 2, 3):
        ag_copy(mine, peer(k, 0)).start()
    sib_copy(mine).start()

    for k_in in (1, 3, 2):
        b = block(0, k_in)
        ag_copy(b, sibling).wait_recv()
        for k in (1, 3, 2):
            ag_copy(b, peer(k, 0)).start()
        sib_copy(b).start()

    def gather_rows(q):
        @pl.loop(0, 4)
        def _(i):
            k_out = q * (1 - c) + i * c

            @pl.when(k_out > 0)
            def _():
                b = block(k_out, i * (1 - c) + q * c)
                ag_copy(b, sibling).wait_recv()
                sib_copy(b).start()

    def sibling_rows(q):
        @pl.loop(0, 4)
        def _(i):
            b = lax.rem(y + q, 4) * 4 + i
            rcopy(full.at[1 - c, b], full.at[1 - c, b], sib_send, sib_recv.at[b], sibling).wait_recv()

    width = full.shape[3]
    hidden_units = chunks * ROWS

    def partial_sums(q):
        for i in range(3):
            acts = full[i // 2, quarter(q)].reshape(128, width)
            sums = lax.dot_general(wt[i], acts, (((1,), (1,)), ((), ())), preferred_element_type=F32)
            part[q, :, i] = sums.astype(BF16).reshape(chunks, ROWS, 128)

    roots = (last, 0, last // 2, last // 2 + 1)

    def red_copy(q, k, side, target):
        return rcopy(part.at[q, k], redbuf.at[side, q, k], red_send.at[q], red_recv.at[side, q, k], (hid, target))

    def bc_copy(q, k, side, target):
        return rcopy(res.at[q, k], res.at[q, k], bc_send.at[side, q], bc_recv.at[q, k], (hid, target))

    def chain_step(step, which):
        for q in which:
            root = roots[q]
            stride = 1 if q < 2 else 2
            base = 0 if q < 2 else chunks
            below = zl < root
            far = (zl == 0) | (zl == last)
            onward = jnp.clip(jnp.where(below, zl + 1, zl - 1), 0, last)
            outward = jnp.clip(jnp.where(below, zl - 1, zl + 1), 0, last)
            side = jnp.where(below, 0, 1)
            root_lag = LAG * max(root, last - root)
            at = step - base - jnp.where(zl == root, root_lag, LAG * jnp.where(below, zl, last - zl))
            k = at // stride
            live = (at >= 0) & (at < chunks * stride) & (lax.rem(at, stride) == 0)

            @pl.when(live & (zl != root))
            def _():
                @pl.when(jnp.logical_not(far))
                def _():
                    red_copy(q, k, side, onward).wait_recv()
                    part[q, k] = (part[q, k].astype(F32) + redbuf[side, q, k].astype(F32)).astype(BF16)

                red_copy(q, k, side, onward).start()

            @pl.when(live & (zl == root))
            def _():
                sums = part[q, k].astype(F32)
                if root > 0:
                    red_copy(q, k, 0, root).wait_recv()
                    sums += redbuf[0, q, k].astype(F32)
                if root < last:
                    red_copy(q, k, 1, root).wait_recv()
                    sums += redbuf[1, q, k].astype(F32)
                hidden, d_gate, d_up = swiglu_grads(sums[0], sums[1], sums[2])
                res[q, k, 0] = hidden
                res[q, k, 1] = d_gate
                res[q, k, 2] = d_up
                if root > 0:
                    bc_copy(q, k, 0, root - 1).start()
                if root < last:
                    bc_copy(q, k, 1, root + 1).start()

            at_b = step - base - root_lag - LAG * jnp.where(below, root - zl, zl - root)
            kb = at_b // stride

            @pl.when((at_b >= 0) & (at_b < chunks * stride) & (lax.rem(at_b, stride) == 0) & (zl != root))
            def _():
                bc_copy(q, kb, 0, zl).wait_recv()

                @pl.when(jnp.logical_not(far))
                def _():
                    bc_copy(q, kb, side, outward).start()

    def chain_steps(start, stop, which):
        @pl.loop(start, stop)
        def _(step):
            chain_step(step, which)

    gather_rows(0)
    gather_rows(1)
    for copy in w_copies:
        copy.wait()
    sibling_rows(0)
    partial_sums(0)
    sibling_rows(1)
    partial_sums(1)
    chain_steps(0, LAG, (0, 1))
    gather_rows(2)
    gather_rows(3)
    chain_steps(LAG, chunks, (0, 1))
    for q in (2, 3):
        sibling_rows(q)
        partial_sums(q)
    chain_steps(chunks, max(chunks + 2 * last * LAG, 3 * chunks + (last + 1) * LAG), (0, 1, 2, 3))

    half = width // 2

    def sib_grad(q):
        return rcopy(
            grad.at[1 - c, quarter(q)], sibbuf.at[quarter(q)], r0_send.at[q], r0_recv.at[q], sibling
        )

    def columns(i, qs):
        return jnp.concatenate([res[q, :, i].reshape(hidden_units, 128) for q in qs], axis=1)

    for qs in ((0, 1), (2, 3)):
        total = jnp.zeros((256, width), F32)
        for i in range(2):
            total += lax.dot_general(columns(i + 1, qs), wt[i], (((0,), (0,)), ((), ())), preferred_element_type=F32)
        total = total.astype(BF16)
        for j, q in enumerate(qs):
            for h in range(2):
                grad[h, quarter(q)] = total[j * 128:(j + 1) * 128, h * half:(h + 1) * half].reshape(4, 32, half)
            sib_grad(q).start()

    def weight_grad(i, scale):
        acts = jnp.concatenate([full[1 if i == 0 else 0, quarter(q)].reshape(128, width) for q in range(4)], axis=0)
        total = jnp.dot(columns(i, range(4)), acts, preferred_element_type=F32)
        if scale is not None:
            total = scale * total
        obuf[i] = total.astype(BF16)
        copy = pltpu.make_async_copy(obuf.at[i], (gd_ref, gg_ref, gu_ref)[i], o_sem.at[i])
        copy.start()
        return copy

    def r1_copy(k_out, k_in):
        return rcopy(
            grad.at[c, block(k_out, k_in)], rb1.at[k_out - 1, k_in],
            r1_send, r1_recv.at[k_out - 1, k_in], peer(k_out, 0),
        )

    def r2_copy(k_in):
        return rcopy(a1.at[k_in], rb2.at[k_in - 1], r2_send, r2_recv.at[k_in - 1], peer(0, k_in))

    for q in range(4):
        rows = quarter(q)
        sib_grad(q).wait_recv()
        grad[c, rows] = (grad[c, rows].astype(F32) + sibbuf[rows].astype(F32)).astype(BF16)

        @pl.loop(0, 4)
        def _(i):
            k_out = q * (1 - c) + i * c

            @pl.when(k_out > 0)
            def _():
                r1_copy(k_out, i * (1 - c) + q * c).start()

    out_copies = [weight_grad(0, readout_scale)]

    for k_in in (1, 2, 3, 0):
        total = grad[c, block(0, k_in)].astype(F32)
        for k_out in (1, 2, 3):
            r1_copy(k_out, k_in).wait_recv()
        for k_out in (1, 2, 3):
            total += rb1[k_out - 1, k_in].astype(F32)
        a1[k_in] = total.astype(BF16)
        if k_in:
            r2_copy(k_in).start()

    out_copies.append(weight_grad(1, None))
    total = a1[0].astype(F32)
    for k_in in (1, 2, 3):
        r2_copy(k_in).wait_recv()
    for k_in in (1, 2, 3):
        total += rb2[k_in - 1].astype(F32)
    a2[...] = total.astype(BF16).reshape(2, 16, half)
    r3 = rcopy(a2.at[1 - z], rb3, r3_send, r3_recv, dev(y, x, 1 - z, c))
    r3.start()
    out_copies.append(weight_grad(2, None))

    for copy in first:
        copy.wait_send()
    rows = pl.ds(0, 15)
    rcopy(full.at[c, rows], full.at[c, rows], ag_send, ag_recv.at[0], sibling).wait_send()
    rcopy(full.at[c], full.at[c], sib_send, sib_recv.at[0], sibling).wait_send()
    for q in range(4):
        root = roots[q]

        @pl.when(zl != root)
        def _():
            rcopy(part.at[q], redbuf.at[0, q], red_send.at[q], red_recv.at[0, q, 0], sibling).wait_send()

        for side in range(2):
            sends = ((zl <= root) & (zl > 0)) if side == 0 else ((zl >= root) & (zl < last))

            @pl.when(sends)
            def _():
                rcopy(res.at[q], res.at[q], bc_send.at[side, q], bc_recv.at[q, 0], sibling).wait_send()

        sib_grad(q).wait_send()
    rows = pl.ds(0, 12)
    rcopy(grad.at[c, rows], sibbuf.at[rows], r1_send, r1_recv.at[0, 0], sibling).wait_send()
    rcopy(rb2, rb2, r2_send, r2_recv.at[0], sibling).wait_send()
    for copy in out_copies:
        copy.wait()

    r3.wait_recv()
    total = a2[z].astype(F32) + rb3[...].astype(F32)
    outbuf[0] = total.reshape(2, 8, half).astype(BF16)
    r4 = rcopy(outbuf.at[0, 1 - c], outbuf.at[1, 0], r4_send, r4_recv, sibling)
    r4.start()
    own = outbuf[0, c]
    r4.wait_recv()
    theirs = outbuf[1, 0]
    is0 = c == 0
    gin_ref[:, :half] = jnp.where(is0, own, theirs)
    gin_ref[:, half:] = jnp.where(is0, theirs, own)
    r3.wait_send()
    r4.wait_send()


def local(tokens, cotangent, gate_weight, up_weight, down_weight):
    width = tokens.shape[1]
    units = down_weight.shape[0]
    chunks = units // ROWS
    half = width // 2
    dma = pltpu.SemaphoreType.DMA
    vmem = pl.BlockSpec(memory_space=pltpu.VMEM)
    hbm = pl.BlockSpec(memory_space=pl.ANY)
    grad_in, grad_gate, grad_up, grad_down = pl.pallas_call(
        kernel,
        out_shape=(
            jax.ShapeDtypeStruct(tokens.shape, BF16),
            jax.ShapeDtypeStruct((units, width), BF16),
            jax.ShapeDtypeStruct((units, width), BF16),
            jax.ShapeDtypeStruct((units, width), BF16),
        ),
        in_specs=[vmem, vmem, hbm, hbm, hbm],
        out_specs=(vmem, hbm, hbm, hbm),
        scratch_shapes=[
            pltpu.VMEM((2, 8, width), BF16),
            pltpu.VMEM((4, 8, width), BF16),
            pltpu.VMEM((2, 16, 32, width), BF16),
            pltpu.VMEM((3, units, width), BF16),
            pltpu.VMEM((4, chunks, 3, ROWS, 128), BF16),
            pltpu.VMEM((2, 4, chunks, 3, ROWS, 128), BF16),
            pltpu.VMEM((4, chunks, 3, ROWS, 128), BF16),
            pltpu.VMEM((2, 16, 32, half), BF16),
            pltpu.VMEM((16, 32, half), BF16),
            pltpu.VMEM((3, 4, 32, half), BF16),
            pltpu.VMEM((4, 32, half), BF16),
            pltpu.VMEM((3, 32, half), BF16),
            pltpu.VMEM((2, 16, half), BF16),
            pltpu.VMEM((16, half), BF16),
            pltpu.VMEM((2, 2, 8, half), BF16),
            pltpu.VMEM((3, units, width), BF16),
            dma((3,)), dma((4,)), dma(()), dma((16,)), dma(()), dma((16,)),
            dma((4,)), dma((2, 4, chunks)), dma((2, 4)), dma((4, chunks)),
            dma((4,)), dma((4,)), dma(()), dma((3, 4)), dma(()), dma((3,)),
            dma(()), dma(()), dma(()), dma(()),
            dma((3,)), dma((3,)),
        ],
        compiler_params=pltpu.CompilerParams(
            collective_id=0, has_side_effects=True, vmem_limit_bytes=56 * 1024 * 1024
        ),
    )(tokens, cotangent, gate_weight.T, up_weight.T, down_weight)
    return grad_in, grad_gate.T, grad_up.T, grad_down


def solution(mesh):
    placed = (P("hid", "mod"), P("hid", "mod"), P("mod", "hid"), P("mod", "hid"), P("hid", "mod"))
    return jax.shard_map(
        local,
        mesh=mesh,
        in_specs=placed,
        out_specs=(P("hid", "mod"), P("mod", "hid"), P("mod", "hid"), P("hid", "mod")),
        check_vma=False,
    )
```

```python
import functools

import jax
import jax.numpy as jnp
from jax import lax
from jax.experimental import pallas as pl
from jax.experimental.pallas import tpu as pltpu
from jax.sharding import PartitionSpec as P

readout_scale = 2.0
N_MOD = 8
LAG = 6
ROWS = 32
MESH = pl.DeviceIdType.MESH
F32 = jnp.float32
BF16 = jnp.bfloat16


def swiglu_grads(gate, up, back):
    back = readout_scale * back
    sigmoid_gate = jax.nn.sigmoid(gate)
    activated = gate * sigmoid_gate
    hidden = (activated * up).astype(BF16)
    d_gate = (back * up * sigmoid_gate * (1.0 + gate * (1.0 - sigmoid_gate))).astype(BF16)
    d_up = (back * activated).astype(BF16)
    return hidden, d_gate, d_up


def kernel(
    tok_ref, cot_ref, wg_ref, wu_ref, wd_ref,
    gin_ref, gg_ref, gu_ref, gd_ref,
    xin, stage, full, wt, part, redbuf, res, grad, sibbuf, rb1, a1, rb2, a2, rb3, outbuf, obuf,
    s0_send, s0_recv, ag_send, ag_recv, sib_send, sib_recv,
    red_send, red_recv, bc_send, bc_recv,
    r0_send, r0_recv, r1_send, r1_recv, r2_send, r2_recv, r3_send, r3_recv, r4_send, r4_recv,
    w_sem, o_sem,
):
    hid = lax.axis_index("hid")
    zl = lax.axis_index("mod")
    c = lax.rem(hid, 2)
    z = lax.rem(hid // 2, 2)
    x = lax.rem(hid // 4, 4)
    y = hid // 16
    chunks = part.shape[1]
    last = N_MOD - 1

    def dev(yy, xx, zz, cc):
        return (((yy * 4 + xx) * 2 + zz) * 2 + cc, zl)

    def coords(k_out, k_in):
        xx = lax.rem(x + k_in * (1 - c) + k_out * c, 4)
        yy = lax.rem(y + k_in * c + k_out * (1 - c), 4)
        return yy, xx

    def block(k_out, k_in):
        yy, xx = coords(k_out, k_in)
        return yy * 4 + xx

    def peer(k_out, k_in):
        yy, xx = coords(k_out, k_in)
        return dev(yy, xx, z, c)

    def half_of(q):
        return z if q < 2 else 1 - z

    def quarter(q):
        return pl.ds(half_of(q) * 16 + (q % 2) * 8, 8)

    def blocks_of(q):
        return pl.ds((q % 2) * 8, 8)

    sibling = dev(y, x, z, 1 - c)

    def rcopy(src, dst, ssem, rsem, target):
        return pltpu.make_async_remote_copy(
            src_ref=src, dst_ref=dst, send_sem=ssem, recv_sem=rsem, device_id=target, device_id_type=MESH
        )

    barrier = pltpu.get_barrier_semaphore()
    greeted = [sibling, dev(y, x, 1 - z, 0), dev(y, x, 1 - z, 1)]
    greeted += [peer(0, k) for k in (1, 2, 3)] + [peer(k, 0) for k in (1, 2, 3)]
    for target in greeted:
        pl.semaphore_signal(barrier, inc=1, device_id=target, device_id_type=MESH)

    @pl.when(zl < last)
    def _():
        pl.semaphore_signal(barrier, inc=1, device_id=(hid, jnp.minimum(zl + 1, last)), device_id_type=MESH)

    @pl.when(zl > 0)
    def _():
        pl.semaphore_signal(barrier, inc=1, device_id=(hid, jnp.maximum(zl - 1, 0)), device_id_type=MESH)

    w_copies = [
        pltpu.make_async_copy(wg_ref, wt.at[0], w_sem.at[0]),
        pltpu.make_async_copy(wu_ref, wt.at[1], w_sem.at[1]),
        pltpu.make_async_copy(wd_ref, wt.at[2], w_sem.at[2]),
    ]
    for copy in w_copies:
        copy.start()
    xin[0] = tok_ref[...]
    xin[1] = cot_ref[...]
    pl.semaphore_wait(barrier, len(greeted) + jnp.minimum(zl, 1) + jnp.minimum(last - zl, 1))

    slot = z * 2 + c
    first = [
        rcopy(xin.at[1 - c], stage.at[slot], s0_send.at[2], s0_recv.at[slot], sibling),
        rcopy(xin.at[0], stage.at[slot], s0_send.at[0], s0_recv.at[slot], dev(y, x, 1 - z, 0)),
        rcopy(xin.at[1], stage.at[slot], s0_send.at[1], s0_recv.at[slot], dev(y, x, 1 - z, 1)),
    ]
    for copy in first:
        copy.start()
    stage[slot] = xin[c]
    mine = y * 4 + x

    def ag_copy(b, target):
        return rcopy(full.at[c, b], full.at[c, b], ag_send, ag_recv.at[b], target)

    def sib_copy(b):
        return rcopy(full.at[c, b], full.at[c, b], sib_send, sib_recv.at[b], sibling)

    def arrived(other):
        rcopy(xin.at[0], stage.at[other], s0_send.at[0], s0_recv.at[other], sibling).wait_recv()

    def begin_half(zz):
        b = zz * 16 + mine
        rows = stage[pl.ds(zz * 2, 2)].astype(F32)
        full[c, b] = rows.reshape(16, stage.shape[2]).astype(BF16)
        for k in (1, 3, 2):
            ag_copy(b, peer(0, k)).start()
        for k in (1, 3, 2):
            ag_copy(b, peer(k, 0)).start()
        sib_copy(b).start()

    def inner_half(zz):
        for k_in in (1, 3, 2):
            b = zz * 16 + block(0, k_in)
            ag_copy(b, sibling).wait_recv()
            for k in (1, 3, 2):
                ag_copy(b, peer(k, 0)).start()
            sib_copy(b).start()

    def outer_half(zz):
        @pl.loop(0, 4)
        def _(k_in):
            for k_out in (1, 3, 2):
                b = zz * 16 + block(k_out, k_in)
                ag_copy(b, sibling).wait_recv()
                sib_copy(b).start()

    def sibling_half(zz):
        @pl.loop(0, 16)
        def _(i):
            b = zz * 16 + i
            rcopy(full.at[1 - c, b], full.at[1 - c, b], sib_send, sib_recv.at[b], sibling).wait_recv()

    width = full.shape[3]
    hidden_units = chunks * ROWS

    width = full.shape[3]
    hidden_units = chunks * ROWS

    def partial_sums(q):
        for i in range(3):
            acts = full[i // 2, quarter(q)].reshape(128, width)
            sums = lax.dot_general(wt[i], acts, (((1,), (1,)), ((), ())), preferred_element_type=F32)
            part[q, :, i] = sums.astype(BF16).reshape(chunks, ROWS, 128)

    roots = (last, 0, last // 2, last // 2 + 1)

    def red_copy(q, k, side, target):
        return rcopy(part.at[q, k], redbuf.at[side, q, k], red_send.at[q], red_recv.at[side, q, k], (hid, target))

    def bc_copy(q, k, side, target):
        return rcopy(res.at[q, k], res.at[q, k], bc_send.at[side, q], bc_recv.at[q, k], (hid, target))

    def chain_step(step, which):
        for q in which:
            root = roots[q]
            stride = 1 if q < 2 else 2
            base = 0 if q < 2 else chunks
            below = zl < root
            far = (zl == 0) | (zl == last)
            onward = jnp.clip(jnp.where(below, zl + 1, zl - 1), 0, last)
            outward = jnp.clip(jnp.where(below, zl - 1, zl + 1), 0, last)
            side = jnp.where(below, 0, 1)
            root_lag = LAG * max(root, last - root)
            at = step - base - jnp.where(zl == root, root_lag, LAG * jnp.where(below, zl, last - zl))
            k = at // stride
            live = (at >= 0) & (at < chunks * stride) & (lax.rem(at, stride) == 0)

            @pl.when(live & (zl != root))
            def _():
                @pl.when(jnp.logical_not(far))
                def _():
                    red_copy(q, k, side, onward).wait_recv()
                    part[q, k] = (part[q, k].astype(F32) + redbuf[side, q, k].astype(F32)).astype(BF16)

                red_copy(q, k, side, onward).start()

            @pl.when(live & (zl == root))
            def _():
                sums = part[q, k].astype(F32)
                if root > 0:
                    red_copy(q, k, 0, root).wait_recv()
                    sums += redbuf[0, q, k].astype(F32)
                if root < last:
                    red_copy(q, k, 1, root).wait_recv()
                    sums += redbuf[1, q, k].astype(F32)
                hidden, d_gate, d_up = swiglu_grads(sums[0], sums[1], sums[2])
                res[q, k, 0] = hidden
                res[q, k, 1] = d_gate
                res[q, k, 2] = d_up
                if root > 0:
                    bc_copy(q, k, 0, root - 1).start()
                if root < last:
                    bc_copy(q, k, 1, root + 1).start()

            at_b = step - base - root_lag - LAG * jnp.where(below, root - zl, zl - root)
            kb = at_b // stride

            @pl.when((at_b >= 0) & (at_b < chunks * stride) & (lax.rem(at_b, stride) == 0) & (zl != root))
            def _():
                bc_copy(q, kb, 0, zl).wait_recv()

                @pl.when(jnp.logical_not(far))
                def _():
                    bc_copy(q, kb, side, outward).start()

    def chain_steps(start, stop, which):
        @pl.loop(start, stop)
        def _(step):
            chain_step(step, which)

    arrived(z * 2 + 1 - c)
    begin_half(z)
    inner_half(z)
    arrived((1 - z) * 2)
    arrived((1 - z) * 2 + 1)
    begin_half(1 - z)
    outer_half(z)
    sibling_half(z)
    inner_half(1 - z)
    for copy in w_copies:
        copy.wait()
    partial_sums(0)
    partial_sums(1)
    chain_steps(0, LAG, (0, 1))
    outer_half(1 - z)
    chain_steps(LAG, chunks, (0, 1))
    sibling_half(1 - z)
    partial_sums(2)
    partial_sums(3)
    chain_steps(chunks, max(chunks + 2 * last * LAG, 3 * chunks + (last + 1) * LAG), (0, 1, 2, 3))

    half = width // 2

    def sib_grad(q):
        return rcopy(
            grad.at[1 - c, blocks_of(q)], sibbuf.at[blocks_of(q)], r0_send.at[q], r0_recv.at[q], sibling
        )

    def columns(i, qs):
        return jnp.concatenate([res[q, :, i].reshape(hidden_units, 128) for q in qs], axis=1)

    for qs in ((0, 2), (1, 3)):
        total = jnp.zeros((256, width), F32)
        for i in range(2):
            total += lax.dot_general(columns(i + 1, qs), wt[i], (((0,), (0,)), ((), ())), preferred_element_type=F32)
        total = total.astype(BF16)
        for j, q in enumerate(qs):
            for h in range(2):
                grad[h, blocks_of(q), half_of(q)] = (
                    total[j * 128:(j + 1) * 128, h * half:(h + 1) * half].reshape(8, 16, half)
                )
        sib_grad(qs[0]).start()

    def weight_grad(i, scale):
        acts = jnp.concatenate([full[1 if i == 0 else 0, quarter(q)].reshape(128, width) for q in range(4)], axis=0)
        total = jnp.dot(columns(i, range(4)), acts, preferred_element_type=F32)
        if scale is not None:
            total = scale * total
        obuf[i] = total.astype(BF16)
        copy = pltpu.make_async_copy(obuf.at[i], (gd_ref, gg_ref, gu_ref)[i], o_sem.at[i])
        copy.start()
        return copy

    def r1_copy(k_out, k_in):
        return rcopy(
            grad.at[c, block(k_out, k_in)], rb1.at[k_out - 1, k_in],
            r1_send, r1_recv.at[k_out - 1, k_in], peer(k_out, 0),
        )

    def r2_copy(k_in):
        return rcopy(a1.at[k_in], rb2.at[k_in - 1], r2_send, r2_recv.at[k_in - 1], peer(0, k_in))

    for q in range(2):
        rows = blocks_of(q)
        sib_grad(q).wait_recv()
        grad[c, rows] = (grad[c, rows].astype(F32) + sibbuf[rows].astype(F32)).astype(BF16)

    for k_in in (1, 2, 3, 0):
        for k_out in (1, 2, 3):
            r1_copy(k_out, k_in).start()

    out_copies = [weight_grad(0, readout_scale)]

    for k_in in (1, 2, 3, 0):
        total = grad[c, block(0, k_in)].astype(F32)
        for k_out in (1, 2, 3):
            r1_copy(k_out, k_in).wait_recv()
        for k_out in (1, 2, 3):
            total += rb1[k_out - 1, k_in].astype(F32)
        a1[k_in] = total.astype(BF16)
        if k_in:
            r2_copy(k_in).start()

    out_copies.append(weight_grad(1, None))
    total = a1[0].astype(F32)
    for k_in in (1, 2, 3):
        r2_copy(k_in).wait_recv()
    for k_in in (1, 2, 3):
        total += rb2[k_in - 1].astype(F32)
    a2[...] = total.astype(BF16)
    r3 = rcopy(a2.at[1 - z], rb3, r3_send, r3_recv, dev(y, x, 1 - z, c))
    r3.start()
    out_copies.append(weight_grad(2, None))

    for copy in first:
        copy.wait_send()
    rows = pl.ds(0, 30)
    rcopy(full.at[c, rows], full.at[c, rows], ag_send, ag_recv.at[0], sibling).wait_send()
    rcopy(full.at[c], full.at[c], sib_send, sib_recv.at[0], sibling).wait_send()
    for q in range(4):
        root = roots[q]

        @pl.when(zl != root)
        def _():
            rcopy(part.at[q], redbuf.at[0, q], red_send.at[q], red_recv.at[0, q, 0], sibling).wait_send()

        for side in range(2):
            sends = ((zl <= root) & (zl > 0)) if side == 0 else ((zl >= root) & (zl < last))

            @pl.when(sends)
            def _():
                rcopy(res.at[q], res.at[q], bc_send.at[side, q], bc_recv.at[q, 0], sibling).wait_send()

    for q in range(2):
        sib_grad(q).wait_send()
    rows = pl.ds(0, 12)
    rcopy(grad.at[c, rows], sibbuf.at[rows], r1_send, r1_recv.at[0, 0], sibling).wait_send()
    rcopy(rb2, rb2, r2_send, r2_recv.at[0], sibling).wait_send()
    for copy in out_copies:
        copy.wait()

    r3.wait_recv()
    total = a2[z].astype(F32) + rb3[...].astype(F32)
    outbuf[0] = total.reshape(2, 8, half).astype(BF16)
    r4 = rcopy(outbuf.at[0, 1 - c], outbuf.at[1, 0], r4_send, r4_recv, sibling)
    r4.start()
    own = outbuf[0, c]
    r4.wait_recv()
    theirs = outbuf[1, 0]
    is0 = c == 0
    gin_ref[:, :half] = jnp.where(is0, own, theirs)
    gin_ref[:, half:] = jnp.where(is0, theirs, own)
    r3.wait_send()
    r4.wait_send()


def local(tokens, cotangent, gate_weight, up_weight, down_weight):
    width = tokens.shape[1]
    units = down_weight.shape[0]
    chunks = units // ROWS
    half = width // 2
    dma = pltpu.SemaphoreType.DMA
    vmem = pl.BlockSpec(memory_space=pltpu.VMEM)
    hbm = pl.BlockSpec(memory_space=pl.ANY)
    grad_in, grad_gate, grad_up, grad_down = pl.pallas_call(
        kernel,
        out_shape=(
            jax.ShapeDtypeStruct(tokens.shape, BF16),
            jax.ShapeDtypeStruct((units, width), BF16),
            jax.ShapeDtypeStruct((units, width), BF16),
            jax.ShapeDtypeStruct((units, width), BF16),
        ),
        in_specs=[vmem, vmem, hbm, hbm, hbm],
        out_specs=(vmem, hbm, hbm, hbm),
        scratch_shapes=[
            pltpu.VMEM((2, 8, width), BF16),
            pltpu.VMEM((4, 8, width), BF16),
            pltpu.VMEM((2, 32, 16, width), BF16),
            pltpu.VMEM((3, units, width), BF16),
            pltpu.VMEM((4, chunks, 3, ROWS, 128), BF16),
            pltpu.VMEM((2, 4, chunks, 3, ROWS, 128), BF16),
            pltpu.VMEM((4, chunks, 3, ROWS, 128), BF16),
            pltpu.VMEM((2, 16, 2, 16, half), BF16),
            pltpu.VMEM((16, 2, 16, half), BF16),
            pltpu.VMEM((3, 4, 2, 16, half), BF16),
            pltpu.VMEM((4, 2, 16, half), BF16),
            pltpu.VMEM((3, 2, 16, half), BF16),
            pltpu.VMEM((2, 16, half), BF16),
            pltpu.VMEM((16, half), BF16),
            pltpu.VMEM((2, 2, 8, half), BF16),
            pltpu.VMEM((3, units, width), BF16),
            dma((3,)), dma((4,)), dma(()), dma((32,)), dma(()), dma((32,)),
            dma((4,)), dma((2, 4, chunks)), dma((2, 4)), dma((4, chunks)),
            dma((2,)), dma((2,)), dma(()), dma((3, 4)), dma(()), dma((3,)),
            dma(()), dma(()), dma(()), dma(()),
            dma((3,)), dma((3,)),
        ],
        compiler_params=pltpu.CompilerParams(
            collective_id=0, has_side_effects=True, vmem_limit_bytes=50 * 1024 * 1024
        ),
    )(tokens, cotangent, gate_weight.T, up_weight.T, down_weight)
    return grad_in, grad_gate.T, grad_up.T, grad_down


def solution(mesh):
    placed = (P("hid", "mod"), P("hid", "mod"), P("mod", "hid"), P("mod", "hid"), P("hid", "mod"))
    return jax.shard_map(
        local,
        mesh=mesh,
        in_specs=placed,
        out_specs=(P("hid", "mod"), P("mod", "hid"), P("mod", "hid"), P("hid", "mod")),
        check_vma=False,
    )
```

```python
import functools

import jax
import jax.numpy as jnp
from jax import lax
from jax.experimental import pallas as pl
from jax.experimental.pallas import tpu as pltpu
from jax.sharding import PartitionSpec as P

readout_scale = 2.0
N_MOD = 8
LAG = 6
ROWS = 32
MESH = pl.DeviceIdType.MESH
F32 = jnp.float32
BF16 = jnp.bfloat16


def swiglu_grads(gate, up, back):
    back = readout_scale * back
    sigmoid_gate = jax.nn.sigmoid(gate)
    activated = gate * sigmoid_gate
    hidden = (activated * up).astype(BF16)
    d_gate = (back * up * sigmoid_gate * (1.0 + gate * (1.0 - sigmoid_gate))).astype(BF16)
    d_up = (back * activated).astype(BF16)
    return hidden, d_gate, d_up


def kernel(
    tok_ref, cot_ref, wg_ref, wu_ref, wd_ref,
    gin_ref, gg_ref, gu_ref, gd_ref,
    xin, stage, full, wt, part, redbuf, res, grad, sibbuf, rb1, a1, rb2, a2, rb3, obuf,
    s0_send, s0_recv, ag_send, ag_recv, sib_send, sib_recv,
    red_send, red_recv, bc_send, bc_recv,
    r0_send, r0_recv, r1_send, r1_recv, r2_send, r2_recv, r3_send, r3_recv,
    w_sem, o_sem,
):
    hid = lax.axis_index("hid")
    zl = lax.axis_index("mod")
    c = lax.rem(hid, 2)
    z = lax.rem(hid // 2, 2)
    x = lax.rem(hid // 4, 4)
    y = hid // 16
    chunks = part.shape[1]
    last = N_MOD - 1

    def dev(yy, xx, zz, cc):
        return (((yy * 4 + xx) * 2 + zz) * 2 + cc, zl)

    def coords(k_out, k_in):
        xx = lax.rem(x + k_in * (1 - c) + k_out * c, 4)
        yy = lax.rem(y + k_in * c + k_out * (1 - c), 4)
        return yy, xx

    def block(k_out, k_in):
        yy, xx = coords(k_out, k_in)
        return yy * 4 + xx

    def peer(k_out, k_in):
        yy, xx = coords(k_out, k_in)
        return dev(yy, xx, z, c)

    def half_of(q):
        return z if q < 2 else 1 - z

    def quarter(q):
        return pl.ds(half_of(q) * 16 + (q % 2) * 8, 8)

    def blocks_of(q):
        return pl.ds((q % 2) * 8, 8)

    sibling = dev(y, x, z, 1 - c)

    def rcopy(src, dst, ssem, rsem, target):
        return pltpu.make_async_remote_copy(
            src_ref=src, dst_ref=dst, send_sem=ssem, recv_sem=rsem, device_id=target, device_id_type=MESH
        )

    x_copies = [
        pltpu.make_async_copy(tok_ref, xin.at[0], w_sem.at[3]),
        pltpu.make_async_copy(cot_ref, xin.at[1], w_sem.at[4]),
    ]
    w_copies = [
        pltpu.make_async_copy(wg_ref, wt.at[0], w_sem.at[0]),
        pltpu.make_async_copy(wu_ref, wt.at[1], w_sem.at[1]),
        pltpu.make_async_copy(wd_ref, wt.at[2], w_sem.at[2]),
    ]
    for copy in x_copies + w_copies:
        copy.start()

    barrier = pltpu.get_barrier_semaphore()
    greeted = [sibling, dev(y, x, 1 - z, 0), dev(y, x, 1 - z, 1)]
    greeted += [peer(0, k) for k in (1, 2, 3)] + [peer(k, 0) for k in (1, 2, 3)]
    for target in greeted:
        pl.semaphore_signal(barrier, inc=1, device_id=target, device_id_type=MESH)

    @pl.when(zl < last)
    def _():
        pl.semaphore_signal(barrier, inc=1, device_id=(hid, jnp.minimum(zl + 1, last)), device_id_type=MESH)

    @pl.when(zl > 0)
    def _():
        pl.semaphore_signal(barrier, inc=1, device_id=(hid, jnp.maximum(zl - 1, 0)), device_id_type=MESH)

    for copy in x_copies:
        copy.wait()
    pl.semaphore_wait(barrier, len(greeted) + jnp.minimum(zl, 1) + jnp.minimum(last - zl, 1))

    slot = z * 2 + c
    first = [
        rcopy(xin.at[1 - c], stage.at[slot], s0_send.at[2], s0_recv.at[slot], sibling),
        rcopy(xin.at[0], stage.at[slot], s0_send.at[0], s0_recv.at[slot], dev(y, x, 1 - z, 0)),
        rcopy(xin.at[1], stage.at[slot], s0_send.at[1], s0_recv.at[slot], dev(y, x, 1 - z, 1)),
    ]
    for copy in first:
        copy.start()
    stage[slot] = xin[c]
    mine = y * 4 + x

    def ag_copy(b, target):
        return rcopy(full.at[c, b], full.at[c, b], ag_send, ag_recv.at[b], target)

    def sib_copy(b):
        return rcopy(full.at[c, b], full.at[c, b], sib_send, sib_recv.at[b], sibling)

    def arrived(other):
        rcopy(xin.at[0], stage.at[other], s0_send.at[0], s0_recv.at[other], sibling).wait_recv()

    def begin_half(zz):
        b = zz * 16 + mine
        rows = stage[pl.ds(zz * 2, 2)].astype(F32)
        full[c, b] = rows.reshape(16, stage.shape[2]).astype(BF16)
        for k in (1, 3, 2):
            ag_copy(b, peer(0, k)).start()
        for k in (1, 3, 2):
            ag_copy(b, peer(k, 0)).start()
        sib_copy(b).start()

    def inner_half(zz):
        for k_in in (1, 3, 2):
            b = zz * 16 + block(0, k_in)
            ag_copy(b, sibling).wait_recv()
            for k in (1, 3, 2):
                ag_copy(b, peer(k, 0)).start()
            sib_copy(b).start()

    def outer_half(zz):
        @pl.loop(0, 4)
        def _(k_in):
            for k_out in (1, 3, 2):
                b = zz * 16 + block(k_out, k_in)
                ag_copy(b, sibling).wait_recv()
                sib_copy(b).start()

    def sibling_half(zz):
        @pl.loop(0, 16)
        def _(i):
            b = zz * 16 + i
            rcopy(full.at[1 - c, b], full.at[1 - c, b], sib_send, sib_recv.at[b], sibling).wait_recv()

    width = full.shape[3]
    hidden_units = chunks * ROWS

    width = full.shape[3]
    hidden_units = chunks * ROWS

    def partial_sums(q):
        for i in range(3):
            acts = full[i // 2, quarter(q)].reshape(128, width)
            sums = lax.dot_general(wt[i], acts, (((1,), (1,)), ((), ())), preferred_element_type=F32)
            part[q, :, i] = sums.astype(BF16).reshape(chunks, ROWS, 128)

    roots = (last, 0, last // 2, last // 2 + 1)

    def red_copy(q, k, side, target):
        return rcopy(part.at[q, k], redbuf.at[side, q, k], red_send.at[q], red_recv.at[side, q, k], (hid, target))

    def bc_copy(q, k, side, target):
        return rcopy(res.at[q, k], res.at[q, k], bc_send.at[side, q], bc_recv.at[q, k], (hid, target))

    def chain_step(step, which):
        for q in which:
            root = roots[q]
            stride = 1 if q < 2 else 2
            base = 0 if q < 2 else chunks
            below = zl < root
            far = (zl == 0) | (zl == last)
            onward = jnp.clip(jnp.where(below, zl + 1, zl - 1), 0, last)
            outward = jnp.clip(jnp.where(below, zl - 1, zl + 1), 0, last)
            side = jnp.where(below, 0, 1)
            root_lag = LAG * max(root, last - root)
            at = step - base - jnp.where(zl == root, root_lag, LAG * jnp.where(below, zl, last - zl))
            k = at // stride
            live = (at >= 0) & (at < chunks * stride) & (lax.rem(at, stride) == 0)

            @pl.when(live & (zl != root))
            def _():
                @pl.when(jnp.logical_not(far))
                def _():
                    red_copy(q, k, side, onward).wait_recv()
                    part[q, k] = (part[q, k].astype(F32) + redbuf[side, q, k].astype(F32)).astype(BF16)

                red_copy(q, k, side, onward).start()

            @pl.when(live & (zl == root))
            def _():
                sums = part[q, k].astype(F32)
                if root > 0:
                    red_copy(q, k, 0, root).wait_recv()
                    sums += redbuf[0, q, k].astype(F32)
                if root < last:
                    red_copy(q, k, 1, root).wait_recv()
                    sums += redbuf[1, q, k].astype(F32)
                hidden, d_gate, d_up = swiglu_grads(sums[0], sums[1], sums[2])
                res[q, k, 0] = hidden
                res[q, k, 1] = d_gate
                res[q, k, 2] = d_up
                if root > 0:
                    bc_copy(q, k, 0, root - 1).start()
                if root < last:
                    bc_copy(q, k, 1, root + 1).start()

            at_b = step - base - root_lag - LAG * jnp.where(below, root - zl, zl - root)
            kb = at_b // stride

            @pl.when((at_b >= 0) & (at_b < chunks * stride) & (lax.rem(at_b, stride) == 0) & (zl != root))
            def _():
                bc_copy(q, kb, 0, zl).wait_recv()

                @pl.when(jnp.logical_not(far))
                def _():
                    bc_copy(q, kb, side, outward).start()

    def chain_steps(start, stop, which):
        @pl.loop(start, stop)
        def _(step):
            chain_step(step, which)

    arrived(z * 2 + 1 - c)
    begin_half(z)
    inner_half(z)
    arrived((1 - z) * 2)
    arrived((1 - z) * 2 + 1)
    begin_half(1 - z)
    outer_half(z)
    sibling_half(z)
    inner_half(1 - z)
    for copy in w_copies:
        copy.wait()
    partial_sums(0)
    partial_sums(1)
    chain_steps(0, LAG, (0, 1))
    outer_half(1 - z)
    chain_steps(LAG, chunks, (0, 1))
    sibling_half(1 - z)
    partial_sums(2)
    partial_sums(3)
    chain_steps(chunks, max(chunks + 2 * last * LAG, 3 * chunks + (last + 1) * LAG), (0, 1, 2, 3))

    half = width // 2

    def sib_grad(q):
        return rcopy(
            grad.at[1 - c, blocks_of(q)], sibbuf.at[blocks_of(q)], r0_send.at[q], r0_recv.at[q], sibling
        )

    def columns(i, qs):
        return jnp.concatenate([res[q, :, i].reshape(hidden_units, 128) for q in qs], axis=1)

    for qs in ((0, 2), (1, 3)):
        total = jnp.zeros((256, width), F32)
        for i in range(2):
            total += lax.dot_general(columns(i + 1, qs), wt[i], (((0,), (0,)), ((), ())), preferred_element_type=F32)
        total = total.astype(BF16)
        for j, q in enumerate(qs):
            for h in range(2):
                grad[h, blocks_of(q), half_of(q)] = (
                    total[j * 128:(j + 1) * 128, h * half:(h + 1) * half].reshape(8, 16, half)
                )
        sib_grad(qs[0]).start()

    def weight_grad(i, scale):
        acts = jnp.concatenate([full[1 if i == 0 else 0, quarter(q)].reshape(128, width) for q in range(4)], axis=0)
        total = jnp.dot(columns(i, range(4)), acts, preferred_element_type=F32)
        if scale is not None:
            total = scale * total
        obuf[i] = total.astype(BF16)
        copy = pltpu.make_async_copy(obuf.at[i], (gd_ref, gg_ref, gu_ref)[i], o_sem.at[i])
        copy.start()
        return copy

    def r1_copy(k_out, k_in):
        return rcopy(
            grad.at[c, block(k_out, k_in)], rb1.at[k_out - 1, k_in],
            r1_send, r1_recv.at[k_out - 1, k_in], peer(k_out, 0),
        )

    def r2_copy(k_in):
        return rcopy(a1.at[k_in], rb2.at[k_in - 1], r2_send, r2_recv.at[k_in - 1], peer(0, k_in))

    for q in range(2):
        rows = blocks_of(q)
        sib_grad(q).wait_recv()
        grad[c, rows] = (grad[c, rows].astype(F32) + sibbuf[rows].astype(F32)).astype(BF16)

        @pl.loop(q * 8, q * 8 + 8)
        def _(b):
            dy = lax.rem(b // 4 + 4 - y, 4)
            dx = lax.rem(lax.rem(b, 4) + 4 - x, 4)
            k_out = dy * (1 - c) + dx * c

            @pl.when(k_out > 0)
            def _():
                r1_copy(k_out, dx * (1 - c) + dy * c).start()

    out_copies = [weight_grad(0, readout_scale)]

    for k_in in (1, 2, 3, 0):
        total = grad[c, block(0, k_in)].astype(F32)
        for k_out in (1, 2, 3):
            r1_copy(k_out, k_in).wait_recv()
        for k_out in (1, 2, 3):
            total += rb1[k_out - 1, k_in].astype(F32)
        a1[k_in] = total.astype(BF16)
        if k_in:
            r2_copy(k_in).start()

    out_copies.append(weight_grad(1, None))
    total = a1[0].astype(F32)
    for k_in in (1, 2, 3):
        r2_copy(k_in).wait_recv()
    for k_in in (1, 2, 3):
        total += rb2[k_in - 1].astype(F32)
    a2[...] = total.reshape(4, 8, half).astype(BF16)
    finals = [
        rcopy(a2.at[(1 - z) * 2], rb3.at[c, 1], r3_send.at[0], r3_recv.at[c, 1], dev(y, x, 1 - z, 0)),
        rcopy(a2.at[(1 - z) * 2 + 1], rb3.at[c, 1], r3_send.at[1], r3_recv.at[c, 1], dev(y, x, 1 - z, 1)),
        rcopy(a2.at[z * 2 + 1 - c], rb3.at[c, 0], r3_send.at[2], r3_recv.at[c, 0], sibling),
    ]
    for copy in finals:
        copy.start()
    rb3[c, 0] = a2[z * 2 + c]
    out_copies.append(weight_grad(2, None))

    for copy in first:
        copy.wait_send()
    rows = pl.ds(0, 30)
    rcopy(full.at[c, rows], full.at[c, rows], ag_send, ag_recv.at[0], sibling).wait_send()
    rcopy(full.at[c], full.at[c], sib_send, sib_recv.at[0], sibling).wait_send()
    for q in range(4):
        root = roots[q]

        @pl.when(zl != root)
        def _():
            rcopy(part.at[q], redbuf.at[0, q], red_send.at[q], red_recv.at[0, q, 0], sibling).wait_send()

        for side in range(2):
            sends = ((zl <= root) & (zl > 0)) if side == 0 else ((zl >= root) & (zl < last))

            @pl.when(sends)
            def _():
                rcopy(res.at[q], res.at[q], bc_send.at[side, q], bc_recv.at[q, 0], sibling).wait_send()

    for q in range(2):
        sib_grad(q).wait_send()
    rows = pl.ds(0, 12)
    rcopy(grad.at[c, rows], sibbuf.at[rows], r1_send, r1_recv.at[0, 0], sibling).wait_send()
    rcopy(rb2, rb2, r2_send, r2_recv.at[0], sibling).wait_send()
    for copy in out_copies:
        copy.wait()

    for h, source in ((1 - c, 0), (0, 1), (1, 1)):
        rcopy(a2.at[0], rb3.at[h, source], r3_send.at[0], r3_recv.at[h, source], sibling).wait_recv()
    for h in range(2):
        total = rb3[h, 0].astype(F32) + rb3[h, 1].astype(F32)
        gin_ref[:, h * half:(h + 1) * half] = total.astype(BF16)
    for copy in finals:
        copy.wait_send()


def local(tokens, cotangent, gate_weight, up_weight, down_weight):
    width = tokens.shape[1]
    units = down_weight.shape[0]
    chunks = units // ROWS
    half = width // 2
    dma = pltpu.SemaphoreType.DMA
    vmem = pl.BlockSpec(memory_space=pltpu.VMEM)
    hbm = pl.BlockSpec(memory_space=pl.ANY)
    grad_in, grad_gate, grad_up, grad_down = pl.pallas_call(
        kernel,
        out_shape=(
            jax.ShapeDtypeStruct(tokens.shape, BF16),
            jax.ShapeDtypeStruct((units, width), BF16),
            jax.ShapeDtypeStruct((units, width), BF16),
            jax.ShapeDtypeStruct((units, width), BF16),
        ),
        in_specs=[hbm] * 5,
        out_specs=(vmem, hbm, hbm, hbm),
        scratch_shapes=[
            pltpu.VMEM((2, 8, width), BF16),
            pltpu.VMEM((4, 8, width), BF16),
            pltpu.VMEM((2, 32, 16, width), BF16),
            pltpu.VMEM((3, units, width), BF16),
            pltpu.VMEM((4, chunks, 3, ROWS, 128), BF16),
            pltpu.VMEM((2, 4, chunks, 3, ROWS, 128), BF16),
            pltpu.VMEM((4, chunks, 3, ROWS, 128), BF16),
            pltpu.VMEM((2, 16, 2, 16, half), BF16),
            pltpu.VMEM((16, 2, 16, half), BF16),
            pltpu.VMEM((3, 4, 2, 16, half), BF16),
            pltpu.VMEM((4, 2, 16, half), BF16),
            pltpu.VMEM((3, 2, 16, half), BF16),
            pltpu.VMEM((4, 8, half), BF16),
            pltpu.VMEM((2, 2, 8, half), BF16),
            pltpu.VMEM((3, units, width), BF16),
            dma((3,)), dma((4,)), dma(()), dma((32,)), dma(()), dma((32,)),
            dma((4,)), dma((2, 4, chunks)), dma((2, 4)), dma((4, chunks)),
            dma((2,)), dma((2,)), dma(()), dma((3, 4)), dma(()), dma((3,)),
            dma((3,)), dma((2, 2)),
            dma((5,)), dma((3,)),
        ],
        compiler_params=pltpu.CompilerParams(
            collective_id=0, has_side_effects=True, vmem_limit_bytes=50 * 1024 * 1024
        ),
    )(*(pltpu.with_memory_space_constraint(a, pltpu.HBM) for a in (tokens, cotangent, gate_weight.T, up_weight.T, down_weight)))
    return grad_in, grad_gate.T, grad_up.T, grad_down


def solution(mesh):
    placed = (P("hid", "mod"), P("hid", "mod"), P("mod", "hid"), P("mod", "hid"), P("hid", "mod"))
    return jax.shard_map(
        local,
        mesh=mesh,
        in_specs=placed,
        out_specs=(P("hid", "mod"), P("mod", "hid"), P("mod", "hid"), P("hid", "mod")),
        check_vma=False,
    )
```

```python
import functools

import jax
import jax.numpy as jnp
from jax import lax
from jax.experimental import pallas as pl
from jax.experimental.pallas import tpu as pltpu
from jax.sharding import PartitionSpec as P

readout_scale = 2.0
N_MOD = 8
LAG = 6
ROWS = 32
MESH = pl.DeviceIdType.MESH
F32 = jnp.float32
BF16 = jnp.bfloat16


def swiglu_grads(gate, up, back):
    back = readout_scale * back
    sigmoid_gate = jax.nn.sigmoid(gate)
    activated = gate * sigmoid_gate
    hidden = (activated * up).astype(BF16)
    d_gate = (back * up * sigmoid_gate * (1.0 + gate * (1.0 - sigmoid_gate))).astype(BF16)
    d_up = (back * activated).astype(BF16)
    return hidden, d_gate, d_up


def kernel(
    tok_ref, cot_ref, wg_ref, wu_ref, wd_ref,
    gin_ref, gg_ref, gu_ref, gd_ref,
    xin, stage, full, wt, part, redbuf, res, grad, sibbuf, rb1, a1, rb2, a2, rb3, obuf,
    s0_send, s0_recv, ag_send, ag_recv, sib_send, sib_recv,
    red_send, red_recv, bc_send, bc_recv,
    r0_send, r0_recv, r1_send, r1_recv, r2_send, r2_recv, r3_send, r3_recv,
    w_sem, o_sem,
):
    hid = lax.axis_index("hid")
    zl = lax.axis_index("mod")
    c = lax.rem(hid, 2)
    z = lax.rem(hid // 2, 2)
    x = lax.rem(hid // 4, 4)
    y = hid // 16
    chunks = part.shape[1]
    last = N_MOD - 1

    def dev(yy, xx, zz, cc):
        return (((yy * 4 + xx) * 2 + zz) * 2 + cc, zl)

    def coords(k_out, k_in):
        xx = lax.rem(x + k_in * (1 - c) + k_out * c, 4)
        yy = lax.rem(y + k_in * c + k_out * (1 - c), 4)
        return yy, xx

    def block(k_out, k_in):
        yy, xx = coords(k_out, k_in)
        return yy * 4 + xx

    def peer(k_out, k_in):
        yy, xx = coords(k_out, k_in)
        return dev(yy, xx, z, c)

    def half_of(q):
        return z if q < 2 else 1 - z

    def quarter(q):
        return pl.ds(half_of(q) * 16 + (q % 2) * 8, 8)

    def blocks_of(q):
        return pl.ds((q % 2) * 8, 8)

    sibling = dev(y, x, z, 1 - c)

    def rcopy(src, dst, ssem, rsem, target):
        return pltpu.make_async_remote_copy(
            src_ref=src, dst_ref=dst, send_sem=ssem, recv_sem=rsem, device_id=target, device_id_type=MESH
        )

    x_copies = [
        pltpu.make_async_copy(tok_ref, xin.at[0], w_sem.at[3]),
        pltpu.make_async_copy(cot_ref, xin.at[1], w_sem.at[4]),
    ]
    w_copies = [
        pltpu.make_async_copy(wg_ref, wt.at[0], w_sem.at[0]),
        pltpu.make_async_copy(wu_ref, wt.at[1], w_sem.at[1]),
        pltpu.make_async_copy(wd_ref, wt.at[2], w_sem.at[2]),
    ]
    for copy in x_copies + w_copies:
        copy.start()

    barrier = pltpu.get_barrier_semaphore()
    greeted = [sibling, dev(y, x, 1 - z, 0), dev(y, x, 1 - z, 1)]
    greeted += [peer(0, k) for k in (1, 2, 3)] + [peer(k, 0) for k in (1, 2, 3)]
    for target in greeted:
        pl.semaphore_signal(barrier, inc=1, device_id=target, device_id_type=MESH)

    @pl.when(zl < last)
    def _():
        pl.semaphore_signal(barrier, inc=1, device_id=(hid, jnp.minimum(zl + 1, last)), device_id_type=MESH)

    @pl.when(zl > 0)
    def _():
        pl.semaphore_signal(barrier, inc=1, device_id=(hid, jnp.maximum(zl - 1, 0)), device_id_type=MESH)

    for copy in x_copies:
        copy.wait()
    pl.semaphore_wait(barrier, len(greeted) + jnp.minimum(zl, 1) + jnp.minimum(last - zl, 1))

    slot = z * 2 + c
    first = [
        rcopy(xin.at[1 - c], stage.at[slot], s0_send.at[2], s0_recv.at[slot], sibling),
        rcopy(xin.at[0], stage.at[slot], s0_send.at[0], s0_recv.at[slot], dev(y, x, 1 - z, 0)),
        rcopy(xin.at[1], stage.at[slot], s0_send.at[1], s0_recv.at[slot], dev(y, x, 1 - z, 1)),
    ]
    for copy in first:
        copy.start()
    stage[slot] = xin[c]
    mine = y * 4 + x

    def ag_copy(b, target):
        return rcopy(full.at[c, b], full.at[c, b], ag_send, ag_recv.at[b], target)

    def sib_copy(b):
        return rcopy(full.at[c, b], full.at[c, b], sib_send, sib_recv.at[b], sibling)

    def arrived(other):
        rcopy(xin.at[0], stage.at[other], s0_send.at[0], s0_recv.at[other], sibling).wait_recv()

    def begin_half(zz):
        b = zz * 16 + mine
        rows = stage[pl.ds(zz * 2, 2)].astype(F32)
        full[c, b] = rows.reshape(16, stage.shape[2]).astype(BF16)
        for k in (1, 3, 2):
            ag_copy(b, peer(0, k)).start()
        for k in (1, 3, 2):
            ag_copy(b, peer(k, 0)).start()
        sib_copy(b).start()

    def inner_half(zz):
        for k_in in (1, 3, 2):
            b = zz * 16 + block(0, k_in)
            ag_copy(b, sibling).wait_recv()
            for k in (1, 3, 2):
                ag_copy(b, peer(k, 0)).start()
            sib_copy(b).start()

    def outer_half(zz):
        @pl.loop(0, 4)
        def _(k_in):
            for k_out in (1, 3, 2):
                b = zz * 16 + block(k_out, k_in)
                ag_copy(b, sibling).wait_recv()
                sib_copy(b).start()

    def sibling_half(zz):
        @pl.loop(0, 16)
        def _(i):
            b = zz * 16 + i
            rcopy(full.at[1 - c, b], full.at[1 - c, b], sib_send, sib_recv.at[b], sibling).wait_recv()

    width = full.shape[3]
    hidden_units = chunks * ROWS

    width = full.shape[3]
    hidden_units = chunks * ROWS

    def partial_sums(q):
        for i in range(3):
            acts = full[i // 2, quarter(q)].reshape(128, width)
            sums = lax.dot_general(wt[i], acts, (((1,), (1,)), ((), ())), preferred_element_type=F32)
            part[q, :, i] = sums.astype(BF16).reshape(chunks, ROWS, 128)

    roots = (last, 0, last // 2, last // 2 + 1)

    def red_copy(q, k, side, target):
        return rcopy(part.at[q, k], redbuf.at[side, q, k], red_send.at[q], red_recv.at[side, q, k], (hid, target))

    def bc_copy(q, k, side, target):
        return rcopy(res.at[q, k], res.at[q, k], bc_send.at[side, q], bc_recv.at[q, k], (hid, target))

    def chain_step(step, which):
        for q in which:
            root = roots[q]
            stride = 1 if q < 2 else 2
            base = 0 if q < 2 else chunks
            below = zl < root
            far = (zl == 0) | (zl == last)
            onward = jnp.clip(jnp.where(below, zl + 1, zl - 1), 0, last)
            outward = jnp.clip(jnp.where(below, zl - 1, zl + 1), 0, last)
            side = jnp.where(below, 0, 1)
            root_lag = LAG * max(root, last - root)
            at = step - base - jnp.where(zl == root, root_lag, LAG * jnp.where(below, zl, last - zl))
            k = at // stride
            live = (at >= 0) & (at < chunks * stride) & (lax.rem(at, stride) == 0)

            @pl.when(live & (zl != root))
            def _():
                @pl.when(jnp.logical_not(far))
                def _():
                    red_copy(q, k, side, onward).wait_recv()
                    part[q, k] = (part[q, k].astype(F32) + redbuf[side, q, k].astype(F32)).astype(BF16)

                red_copy(q, k, side, onward).start()

            @pl.when(live & (zl == root))
            def _():
                sums = part[q, k].astype(F32)
                if root > 0:
                    red_copy(q, k, 0, root).wait_recv()
                    sums += redbuf[0, q, k].astype(F32)
                if root < last:
                    red_copy(q, k, 1, root).wait_recv()
                    sums += redbuf[1, q, k].astype(F32)
                hidden, d_gate, d_up = swiglu_grads(sums[0], sums[1], sums[2])
                res[q, k, 0] = hidden
                res[q, k, 1] = d_gate
                res[q, k, 2] = d_up
                if root > 0:
                    bc_copy(q, k, 0, root - 1).start()
                if root < last:
                    bc_copy(q, k, 1, root + 1).start()

            at_b = step - base - root_lag - LAG * jnp.where(below, root - zl, zl - root)
            kb = at_b // stride

            @pl.when((at_b >= 0) & (at_b < chunks * stride) & (lax.rem(at_b, stride) == 0) & (zl != root))
            def _():
                bc_copy(q, kb, 0, zl).wait_recv()

                @pl.when(jnp.logical_not(far))
                def _():
                    bc_copy(q, kb, side, outward).start()

    def chain_steps(start, stop, which):
        @pl.loop(start, stop)
        def _(step):
            chain_step(step, which)

    arrived(z * 2 + 1 - c)
    begin_half(z)
    inner_half(z)
    arrived((1 - z) * 2)
    arrived((1 - z) * 2 + 1)
    begin_half(1 - z)
    outer_half(z)
    sibling_half(z)
    for copy in w_copies:
        copy.wait()
    partial_sums(0)
    partial_sums(1)
    chain_steps(0, LAG // 2, (0, 1))
    inner_half(1 - z)
    chain_steps(LAG // 2, LAG + 2, (0, 1))
    outer_half(1 - z)
    chain_steps(LAG + 2, chunks, (0, 1))
    sibling_half(1 - z)
    partial_sums(2)
    partial_sums(3)
    chain_steps(chunks, max(chunks + 2 * last * LAG, 3 * chunks + (last + 1) * LAG), (0, 1, 2, 3))

    half = width // 2

    def sib_grad(q):
        return rcopy(
            grad.at[1 - c, blocks_of(q)], sibbuf.at[blocks_of(q)], r0_send.at[q], r0_recv.at[q], sibling
        )

    def columns(i, qs):
        return jnp.concatenate([res[q, :, i].reshape(hidden_units, 128) for q in qs], axis=1)

    for qs in ((0, 2), (1, 3)):
        total = jnp.zeros((256, width), F32)
        for i in range(2):
            total += lax.dot_general(columns(i + 1, qs), wt[i], (((0,), (0,)), ((), ())), preferred_element_type=F32)
        total = total.astype(BF16)
        for j, q in enumerate(qs):
            for h in range(2):
                grad[h, blocks_of(q), half_of(q)] = (
                    total[j * 128:(j + 1) * 128, h * half:(h + 1) * half].reshape(8, 16, half)
                )
        sib_grad(qs[0]).start()

    def weight_grad(i, scale):
        acts = jnp.concatenate([full[1 if i == 0 else 0, quarter(q)].reshape(128, width) for q in range(4)], axis=0)
        total = jnp.dot(columns(i, range(4)), acts, preferred_element_type=F32)
        if scale is not None:
            total = scale * total
        obuf[i] = total.astype(BF16)
        copy = pltpu.make_async_copy(obuf.at[i], (gd_ref, gg_ref, gu_ref)[i], o_sem.at[i])
        copy.start()
        return copy

    def r1_copy(k_out, k_in):
        return rcopy(
            grad.at[c, block(k_out, k_in)], rb1.at[k_out - 1, k_in],
            r1_send, r1_recv.at[k_out - 1, k_in], peer(k_out, 0),
        )

    def r2_copy(k_in):
        return rcopy(a1.at[k_in], rb2.at[k_in - 1], r2_send, r2_recv.at[k_in - 1], peer(0, k_in))

    for q in range(2):
        rows = blocks_of(q)
        sib_grad(q).wait_recv()
        grad[c, rows] = (grad[c, rows].astype(F32) + sibbuf[rows].astype(F32)).astype(BF16)

        @pl.loop(q * 8, q * 8 + 8)
        def _(b):
            dy = lax.rem(b // 4 + 4 - y, 4)
            dx = lax.rem(lax.rem(b, 4) + 4 - x, 4)
            k_out = dy * (1 - c) + dx * c

            @pl.when(k_out > 0)
            def _():
                r1_copy(k_out, dx * (1 - c) + dy * c).start()

    out_copies = [weight_grad(0, readout_scale)]

    for k_in in (1, 2, 3, 0):
        total = grad[c, block(0, k_in)].astype(F32)
        for k_out in (1, 2, 3):
            r1_copy(k_out, k_in).wait_recv()
        for k_out in (1, 2, 3):
            total += rb1[k_out - 1, k_in].astype(F32)
        a1[k_in] = total.astype(BF16)
        if k_in:
            r2_copy(k_in).start()

    total = a1[0].astype(F32)
    for k_in in (1, 2, 3):
        r2_copy(k_in).wait_recv()
    for k_in in (1, 2, 3):
        total += rb2[k_in - 1].astype(F32)
    a2[...] = total.reshape(4, 8, half).astype(BF16)
    finals = [
        rcopy(a2.at[(1 - z) * 2], rb3.at[c, 1], r3_send.at[0], r3_recv.at[c, 1], dev(y, x, 1 - z, 0)),
        rcopy(a2.at[(1 - z) * 2 + 1], rb3.at[c, 1], r3_send.at[1], r3_recv.at[c, 1], dev(y, x, 1 - z, 1)),
        rcopy(a2.at[z * 2 + 1 - c], rb3.at[c, 0], r3_send.at[2], r3_recv.at[c, 0], sibling),
    ]
    for copy in finals:
        copy.start()
    rb3[c, 0] = a2[z * 2 + c]
    out_copies.append(weight_grad(1, None))
    out_copies.append(weight_grad(2, None))

    for copy in first:
        copy.wait_send()
    rows = pl.ds(0, 30)
    rcopy(full.at[c, rows], full.at[c, rows], ag_send, ag_recv.at[0], sibling).wait_send()
    rcopy(full.at[c], full.at[c], sib_send, sib_recv.at[0], sibling).wait_send()
    for q in range(4):
        root = roots[q]

        @pl.when(zl != root)
        def _():
            rcopy(part.at[q], redbuf.at[0, q], red_send.at[q], red_recv.at[0, q, 0], sibling).wait_send()

        for side in range(2):
            sends = ((zl <= root) & (zl > 0)) if side == 0 else ((zl >= root) & (zl < last))

            @pl.when(sends)
            def _():
                rcopy(res.at[q], res.at[q], bc_send.at[side, q], bc_recv.at[q, 0], sibling).wait_send()

    for q in range(2):
        sib_grad(q).wait_send()
    rows = pl.ds(0, 12)
    rcopy(grad.at[c, rows], sibbuf.at[rows], r1_send, r1_recv.at[0, 0], sibling).wait_send()
    rcopy(rb2, rb2, r2_send, r2_recv.at[0], sibling).wait_send()
    for copy in out_copies:
        copy.wait()

    for h, source in ((1 - c, 0), (0, 1), (1, 1)):
        rcopy(a2.at[0], rb3.at[h, source], r3_send.at[0], r3_recv.at[h, source], sibling).wait_recv()
    for h in range(2):
        total = rb3[h, 0].astype(F32) + rb3[h, 1].astype(F32)
        gin_ref[:, h * half:(h + 1) * half] = total.astype(BF16)
    for copy in finals:
        copy.wait_send()


def local(tokens, cotangent, gate_weight, up_weight, down_weight):
    width = tokens.shape[1]
    units = down_weight.shape[0]
    chunks = units // ROWS
    half = width // 2
    dma = pltpu.SemaphoreType.DMA
    vmem = pl.BlockSpec(memory_space=pltpu.VMEM)
    hbm = pl.BlockSpec(memory_space=pl.ANY)
    grad_in, grad_gate, grad_up, grad_down = pl.pallas_call(
        kernel,
        out_shape=(
            jax.ShapeDtypeStruct(tokens.shape, BF16),
            jax.ShapeDtypeStruct((units, width), BF16),
            jax.ShapeDtypeStruct((units, width), BF16),
            jax.ShapeDtypeStruct((units, width), BF16),
        ),
        in_specs=[hbm] * 5,
        out_specs=(vmem, hbm, hbm, hbm),
        scratch_shapes=[
            pltpu.VMEM((2, 8, width), BF16),
            pltpu.VMEM((4, 8, width), BF16),
            pltpu.VMEM((2, 32, 16, width), BF16),
            pltpu.VMEM((3, units, width), BF16),
            pltpu.VMEM((4, chunks, 3, ROWS, 128), BF16),
            pltpu.VMEM((2, 4, chunks, 3, ROWS, 128), BF16),
            pltpu.VMEM((4, chunks, 3, ROWS, 128), BF16),
            pltpu.VMEM((2, 16, 2, 16, half), BF16),
            pltpu.VMEM((16, 2, 16, half), BF16),
            pltpu.VMEM((3, 4, 2, 16, half), BF16),
            pltpu.VMEM((4, 2, 16, half), BF16),
            pltpu.VMEM((3, 2, 16, half), BF16),
            pltpu.VMEM((4, 8, half), BF16),
            pltpu.VMEM((2, 2, 8, half), BF16),
            pltpu.VMEM((3, units, width), BF16),
            dma((3,)), dma((4,)), dma(()), dma((32,)), dma(()), dma((32,)),
            dma((4,)), dma((2, 4, chunks)), dma((2, 4)), dma((4, chunks)),
            dma((2,)), dma((2,)), dma(()), dma((3, 4)), dma(()), dma((3,)),
            dma((3,)), dma((2, 2)),
            dma((5,)), dma((3,)),
        ],
        compiler_params=pltpu.CompilerParams(
            collective_id=0, has_side_effects=True, vmem_limit_bytes=50 * 1024 * 1024
        ),
    )(*(pltpu.with_memory_space_constraint(a, pltpu.HBM) for a in (tokens, cotangent, gate_weight.T, up_weight.T, down_weight)))
    return grad_in, grad_gate.T, grad_up.T, grad_down


def solution(mesh):
    placed = (P("hid", "mod"), P("hid", "mod"), P("mod", "hid"), P("mod", "hid"), P("hid", "mod"))
    return jax.shard_map(
        local,
        mesh=mesh,
        in_specs=placed,
        out_specs=(P("hid", "mod"), P("mod", "hid"), P("mod", "hid"), P("hid", "mod")),
        check_vma=False,
    )
```
